32 devices in a mesh: group: 4 (over z), dev: 8 (over y, x, core).
Axes of the slice: x: 2, y: 2, z: 4, core: 2. Of those that a mesh axis runs over, the one named last changes fastest.
Arguments:
- tile_values: bfloat16 [512, 128, 128], P(('group', 'dev')), may hold values from -0.25 to 0.25
- tile_rows: int32 [512], P(('group', 'dev')), may hold values from 0 to 1
- tile_columns: int32 [512], P(('group', 'dev')), may hold values from 0 to 15
- tile_count: int32 [32], P(('group', 'dev')), may hold values from 4 to 16, as said below
- start_basis: bfloat16 [8192, 64], P(('group', 'dev')), may hold values from -6 to 6
- seed_rows: int32 [1024], replicated, may hold values from 0 to 8191
Outputs:
- unit_embedding: float32 [8192, 64], P(('group', 'dev'))
- centroids: float32 [1024, 64], replicated
The draws below stay inside these ranges and needn't reach their ends.
Inputs may be any that keep to these rules, and one draw needn't show every extreme that they name: `tile_count`: the most, 16, is reached by some device in every draw.
All inputs are finite; a program needn't handle non-finite values.
Results may differ from the reference program's by a relative error of at most 0.0029.
Values may be sent and summed in bfloat16 or wider, within the bound.
A program may use at most 64 MiB of HBM per device.

```python
import jax
import jax.numpy as jnp
from jax import lax

BLOCK = 128
BASIS = 64
CLUSTERS = 1024
ROWS_DEV = 256
TILES_MAX = 16
ITERS = 2
KSTEPS = 2
ROW_BLOCKS = 2
GROUP_BLOCKS = 16
NROWS = 8192
N_GROUP = 4
N_DEV = 8
DEVICES = 32


def draw_tile_count(key, part):
    first_key, second_key, third_key = jax.random.split(jax.random.fold_in(key, 17), 3)
    device_total = N_GROUP * N_DEV
    base = jax.random.randint(first_key, (device_total,), TILES_MAX // 4, TILES_MAX // 2 + 1)
    full = jax.random.randint(second_key, (device_total,), 0, 8) == 0
    counts = jnp.where(full, TILES_MAX, base)
    chosen = jax.random.randint(third_key, (), 0, device_total)
    return counts.at[chosen].set(TILES_MAX).astype(jnp.int32)


def touch_ends(array, key, smallest, top_value):
    place = [jax.random.randint(jax.random.fold_in(key, axis), (), 0, length) for axis, length in enumerate(array.shape)]
    main_axis = array.shape.index(max(array.shape))
    beside = place[:main_axis] + [(place[main_axis] + 1) % array.shape[main_axis]] + place[main_axis + 1:]
    return array.at[tuple(place)].set(smallest).at[tuple(beside)].set(top_value)


def block_scale(stream_key, shape, cuts, least, top_value):
    factor_of = 1.0
    for dim, blocks in cuts:
        draws = jax.random.uniform(jax.random.fold_in(jax.random.fold_in(stream_key, 6), dim), (blocks,), jnp.float32, least / len(cuts), top_value / len(cuts))
        factor_of = factor_of * jnp.repeat(jnp.exp(draws), shape[dim] // blocks).reshape((-1,) + (1,) * (len(shape) - 1 - dim))
    return factor_of


def gaussian(rng, shape, width, most, pieces=(), kind=jnp.bfloat16):
    array = jax.random.normal(rng, shape, jnp.float32) * width
    if len(pieces) > 0:
        array = block_scale(rng, shape, pieces, -0.22, 0.18) * array
    return jnp.clip(array, min=-most, max=most).astype(kind)


def setup_inputs(seed: int = 0) -> dict:
    arg_keys = jax.random.split(jax.random.key(seed), 7)
    tile_values = gaussian(arg_keys[0], (DEVICES * TILES_MAX, BLOCK, BLOCK), (4 * BLOCK) ** -0.5, 0.25, ((0, 32),))
    tile_rows = touch_ends(jax.random.randint(arg_keys[1], (DEVICES * TILES_MAX,), 0, ROW_BLOCKS), jax.random.fold_in(arg_keys[1], 1), 0, ROW_BLOCKS - 1).astype(jnp.int32)
    tile_columns = touch_ends(jax.random.randint(arg_keys[2], (DEVICES * TILES_MAX,), 0, GROUP_BLOCKS), jax.random.fold_in(arg_keys[2], 1), 0, GROUP_BLOCKS - 1).astype(jnp.int32)
    tile_count = draw_tile_count(jax.random.fold_in(arg_keys[6], 71), 0)
    start_basis = gaussian(arg_keys[4], (NROWS, BASIS), 1.0, 6.0, ((0, 32),))
    seed_rows = touch_ends(jax.random.randint(arg_keys[5], (CLUSTERS,), 0, NROWS), jax.random.fold_in(arg_keys[5], 1), 0, NROWS - 1).astype(jnp.int32)
    return {"tile_values": tile_values, "tile_rows": tile_rows, "tile_columns": tile_columns, "tile_count": tile_count, "start_basis": start_basis, "seed_rows": seed_rows}


def apply_tiles(tile_block, row_index, column_index, live_count, group_basis):
    basis_blocks = group_basis.reshape(-1, BLOCK, BASIS)
    picked = jnp.take(basis_blocks, column_index, axis=0)
    products = jnp.einsum('tij,tjk->tik', tile_block.astype(jnp.float32), picked.astype(jnp.float32))
    live = jnp.arange(TILES_MAX, dtype=jnp.int32) < live_count
    block_index = jnp.arange(ROWS_DEV // BLOCK, dtype=jnp.int32)
    select = ((row_index[None, :] == block_index[:, None]) & live[None, :]).astype(jnp.float32)
    total = jnp.einsum('rt,tik->rik', select, products)
    return total.reshape(ROWS_DEV, BASIS)

def reference(tile_values, tile_rows, tile_columns, tile_count, start_basis, seed_rows):
    device_total = N_GROUP * N_DEV
    tiles_each = tile_values.reshape(device_total, TILES_MAX, BLOCK, BLOCK)
    rows_each = tile_rows.reshape(device_total, TILES_MAX)
    columns_each = tile_columns.reshape(device_total, TILES_MAX)
    basis = start_basis
    embedding = None
    for step_index in range(ITERS):
        group_basis = basis.reshape(N_GROUP, N_DEV * ROWS_DEV, BASIS)

        def one_device(device):
            return apply_tiles(tiles_each[device], rows_each[device], columns_each[device], tile_count[device], group_basis[device // N_DEV])
        image = lax.map(one_device, jnp.arange(device_total, dtype=jnp.int32)).reshape(NROWS, BASIS)
        gram = jnp.dot(image.T, image, precision=lax.Precision.HIGHEST)
        lower = jnp.linalg.cholesky(gram)
        solved = lax.linalg.triangular_solve(lower, image, left_side=False, lower=True, transpose_a=True)
        if step_index + 1 < ITERS:
            basis = solved.astype(jnp.bfloat16)
        else:
            embedding = solved * jnp.sqrt(jnp.float32(NROWS))
    unit = embedding / jnp.sqrt(lax.optimization_barrier(jnp.sum(embedding * embedding, axis=1, keepdims=True)) + 1e-06)
    centres = unit[seed_rows]
    unit_blocks = unit.reshape(-1, ROWS_DEV, BASIS)
    for kstep in range(KSTEPS):
        centre_square = lax.optimization_barrier(jnp.sum(centres * centres, axis=1))

        def accumulate(carry, rows_block):
            weighted, mass = carry
            dist = lax.optimization_barrier(jnp.sum(rows_block * rows_block, axis=1))[:, None] - 2.0 * jnp.dot(rows_block, centres.T, precision=lax.Precision.HIGHEST) + centre_square[None, :]
            weights = jnp.exp(-4.0 * dist)
            member = weights / lax.optimization_barrier(jnp.sum(weights, axis=1, keepdims=True))
            weighted = weighted + jnp.dot(member.T, rows_block, precision=lax.Precision.HIGHEST)
            mass = mass + lax.optimization_barrier(jnp.sum(member, axis=0))
            return ((weighted, mass), None)
        start = (jnp.zeros((CLUSTERS, BASIS), jnp.float32), jnp.zeros((CLUSTERS,), jnp.float32))
        (weighted, mass), unused = lax.scan(accumulate, start, unit_blocks)
        centres = weighted / mass[:, None]
    return (unit, centres)
```

```python
import functools

import jax
import jax.numpy as jnp
from jax import lax
from jax.experimental import pallas as pl
from jax.experimental.pallas import tpu as pltpu
from jax.sharding import PartitionSpec as P

KSTEPS = 2
SHARPNESS = 4.0
MESH = pl.DeviceIdType.MESH
F32 = jnp.float32
HIGHEST = lax.Precision.HIGHEST
NN = (((1,), (0,)), ((), ()))
NT = (((1,), (1,)), ((), ()))


def mm(a, b, dims=NN):
    return lax.dot_general(a, b, dims, precision=HIGHEST, preferred_element_type=F32)


def loop(n, body):
    if n <= 8:
        for i in range(n):
            body(i)
    else:

        def step(i, carry):
            body(i)
            return carry

        lax.fori_loop(0, n, step, 0)


def fold(n, ref):
    if n <= 8:
        total = ref[0]
        for i in range(1, n):
            total = total + ref[i]
        return total
    return lax.fori_loop(1, n, lambda i, total: total + ref[i], ref[0])


class Exchange:
    def __init__(self, axis, n, me, land, sems, source=None):
        self.axis, self.n, self.me = axis, n, me
        self.land, self.source = land, source
        self.send, self.recv = sems

    def copy(self, peer, slot):
        source = self.land(self.me) if self.source is None else self.source(peer)
        return pltpu.make_async_remote_copy(
            src_ref=source,
            dst_ref=self.land(slot),
            send_sem=self.send.at[peer],
            recv_sem=self.recv.at[slot],
            device_id={self.axis: peer},
            device_id_type=MESH,
        )

    def peer(self, i):
        return lax.rem(self.me + 1 + i, self.n)

    def start(self):
        loop(self.n - 1, lambda i: self.copy(self.peer(i), self.me).start())

    def wait_recv(self):
        loop(self.n - 1, lambda i: self.copy(self.peer(i), self.peer(i)).wait_recv())

    def wait_send(self):
        loop(self.n - 1, lambda i: self.copy(self.peer(i), self.me).wait_send())


def factor_inverse(gram):
    k = gram.shape[0]
    rows = lax.broadcasted_iota(jnp.int32, (k, k), 0)
    lanes = lax.broadcasted_iota(jnp.int32, (k, k), 1)
    table = jnp.concatenate([gram, jnp.where(rows == lanes, 1.0, 0.0).astype(F32)], axis=1)
    parts = [table[8 * b : 8 * b + 8] for b in range(k // 8)]
    sub = lax.broadcasted_iota(jnp.int32, (8, 2 * k), 0)
    for i in range(k):
        b, r = divmod(i, 8)
        row = parts[b][r : r + 1]
        scaled = row / row[:, i : i + 1]
        own = parts[b] - parts[b][:, i : i + 1] * scaled
        if r < 7:
            parts[b] = jnp.where(sub > r, own, parts[b])
        for c in range(b + 1, k // 8):
            parts[c] = parts[c] - parts[c][:, i : i + 1] * scaled
    table = jnp.concatenate(parts, axis=0)
    diag = jnp.sum(jnp.where(rows == lanes, table[:, :k], 0.0), axis=1, keepdims=True)
    return table[:, k:] / jnp.sqrt(diag)


def pack(gram):
    half = gram.shape[0] // 2
    return jnp.concatenate([gram[:half], gram[half:]], axis=1)


def unpack(packed):
    k = packed.shape[1] // 2
    return jnp.concatenate([packed[:, :k], packed[:, k:]], axis=0)


def kernel(
    n, m, total_rows,
    tiles, rows_ref, columns_ref, count_ref, start, seeds,
    unit_out, centres_out,
    matrix, basis0, basis1, images, gram_dev, gram_group,
    seed_out, seed_dev, seed_group, seed_all,
    k_out, k_dev, k_group, k_all,
    *sems,
):
    me, g = lax.axis_index("dev"), lax.axis_index("group")
    pairs = [(sems[2 * i], sems[2 * i + 1]) for i in range(len(sems) // 2)]
    slots, block = tiles.shape[0], tiles.shape[1]
    local_rows, width = start.shape
    row_blocks = local_rows // block
    clusters = seeds.shape[1]
    part = clusters // n

    barrier = pltpu.get_barrier_semaphore()
    for axis, size, index in (("dev", n, me), ("group", m, g)):
        loop(
            size - 1,
            lambda i: pl.semaphore_signal(
                barrier, inc=1, device_id={axis: lax.rem(index + 1 + i, size)}, device_id_type=MESH
            ),
        )
    eye = jnp.where(
        lax.broadcasted_iota(jnp.int32, (width, width), 0)
        == lax.broadcasted_iota(jnp.int32, (width, width), 1),
        1.0,
        0.0,
    ).astype(jnp.bfloat16)
    start_t = lax.dot_general(eye, start[...], NT, preferred_element_type=F32)
    for r in range(row_blocks):
        basis0[me * row_blocks + r] = start_t[:, r * block : (r + 1) * block].astype(jnp.bfloat16)
    pl.semaphore_wait(barrier, n - 1 + m - 1)

    used = iter(pairs)
    pending = []

    def exchange(axis, land, source=None):
        size, index = (n, me) if axis == "dev" else (m, g)
        made = Exchange(axis, size, index, land, next(used), source)
        made.start()
        pending.append(made)
        return made

    own_blocks = lambda d: basis0.at[pl.ds(d * row_blocks, row_blocks)]
    gather = exchange("dev", own_blocks)
    count = count_ref[0]
    for s in range(slots):
        for r in range(row_blocks):
            keep = jnp.logical_and(rows_ref[s] == r, s < count)
            matrix[r * block : (r + 1) * block, s * block : (s + 1) * block] = tiles[s] * jnp.where(
                keep, 1.0, 0.0
            ).astype(jnp.bfloat16)

    def apply(basis):
        picked = jnp.concatenate([basis[columns_ref[s]] for s in range(slots)], axis=1)
        return lax.dot_general(picked, matrix[...], NT, preferred_element_type=F32)

    def start_gram(image, turn):
        gram_dev[turn, me] = pack(mm(image, image, NT))
        return exchange("dev", lambda d: gram_dev.at[turn, d])

    def end_gram(first, turn):
        first.wait_recv()
        gram_group[turn, g] = fold(n, gram_dev.at[turn])
        return exchange("group", lambda d: gram_group.at[turn, d])

    gather.wait_recv()
    image = apply(basis0)
    first = start_gram(image, 0)
    images[me] = image
    gather = exchange("dev", lambda d: images.at[d])
    second = end_gram(first, 0)
    second.wait_recv()
    inverse = factor_inverse(unpack(fold(m, gram_group.at[0])))
    gather.wait_recv()

    def solve(d):
        solved = mm(inverse, images[d])
        for r in range(row_blocks):
            basis1[d * row_blocks + r] = solved[:, r * block : (r + 1) * block].astype(jnp.bfloat16)

    loop(n, solve)
    image = apply(basis1)
    first = start_gram(image, 1)

    def split(values, out, lo, hi):
        for c in range(n):
            out[c, lo:hi] = values[:, c * part : (c + 1) * part]

    def join(ref):
        return jnp.concatenate([ref[c] for c in range(n)], axis=1)

    first_row = (g * n + me) * local_rows
    chooser = jnp.where(
        lax.broadcasted_iota(jnp.int32, (local_rows, clusters), 0) == seeds[...] - first_row, 1.0, 0.0
    ).astype(F32)
    split(mm(image, chooser), seed_out, 0, width)
    seed_dev[me] = seed_out[me]
    reduce_dev = exchange("dev", lambda d: seed_dev.at[d], lambda p: seed_out.at[p])
    second = end_gram(first, 1)
    reduce_dev.wait_recv()
    seed_group[g] = fold(n, seed_dev)
    reduce_group = exchange("group", lambda d: seed_group.at[d])
    second.wait_recv()
    packed = fold(m, gram_group.at[1])
    reduce_group.wait_recv()
    seed_all[me] = fold(m, seed_group)
    gather = exchange("dev", lambda d: seed_all.at[d])
    inverse = factor_inverse(unpack(packed))

    def normalise(image_t):
        embedding = mm(inverse, image_t) * jnp.sqrt(F32(total_rows))
        return embedding / jnp.sqrt(jnp.sum(embedding * embedding, axis=0, keepdims=True) + 1e-06)

    unit_t = normalise(image)
    unit = unit_t.T
    unit_out[...] = unit
    unit_square = jnp.sum(unit * unit, axis=1, keepdims=True)
    gather.wait_recv()
    centres = normalise(join(seed_all))
    for turn in range(KSTEPS):
        dist = unit_square - 2.0 * mm(unit, centres) + jnp.sum(centres * centres, axis=0, keepdims=True)
        weights = jnp.exp(-SHARPNESS * dist)
        member = weights / jnp.sum(weights, axis=1, keepdims=True)
        split(mm(unit_t, member), k_out.at[turn], 0, width)
        mass = jnp.sum(member, axis=0, keepdims=True)
        split(jnp.broadcast_to(mass, (8, clusters)), k_out.at[turn], width, width + 8)
        k_dev[turn, me] = k_out[turn, me]
        reduce_dev = exchange(
            "dev", lambda d: k_dev.at[turn, d], lambda p: k_out.at[turn, p]
        )
        reduce_dev.wait_recv()
        k_group[turn, g] = fold(n, k_dev.at[turn])
        reduce_group = exchange("group", lambda d: k_group.at[turn, d])
        reduce_group.wait_recv()
        sums = fold(m, k_group.at[turn])
        k_all[turn, me] = sums[:width] / sums[width : width + 1]
        gather = exchange("dev", lambda d: k_all.at[turn, d])
        gather.wait_recv()
        centres = join(k_all.at[turn])
    centres_out[...] = centres.T
    for made in pending:
        made.wait_send()


def local(tile_values, tile_rows, tile_columns, tile_count, start_basis, seed_rows):
    n, m = lax.axis_size("dev"), lax.axis_size("group")
    slots, block = tile_values.shape[0], tile_values.shape[1]
    local_rows, width = start_basis.shape
    row_blocks = local_rows // block
    clusters = seed_rows.shape[0]
    part = clusters // n
    vmem = pl.BlockSpec(memory_space=pltpu.VMEM)
    smem = pl.BlockSpec(memory_space=pltpu.SMEM)
    half = (width // 2, 2 * width)
    axes = ["dev", "dev", "dev", "group", "dev", "dev", "group", "group", "dev"]
    axes += ["dev", "group", "dev"] * KSTEPS
    sems = []
    for axis in axes:
        sems += [pltpu.SemaphoreType.DMA((n if axis == "dev" else m,))] * 2
    return pl.pallas_call(
        functools.partial(kernel, n, m, local_rows * n * m),
        out_shape=(
            jax.ShapeDtypeStruct((local_rows, width), F32),
            jax.ShapeDtypeStruct((clusters, width), F32),
        ),
        in_specs=[vmem, smem, smem, smem, vmem, vmem],
        out_specs=(vmem, vmem),
        scratch_shapes=[
            pltpu.VMEM((local_rows, slots * block), jnp.bfloat16),
            pltpu.VMEM((n * row_blocks, width, block), jnp.bfloat16),
            pltpu.VMEM((n * row_blocks, width, block), jnp.bfloat16),
            pltpu.VMEM((n, width, local_rows), F32),
            pltpu.VMEM((2, n, *half), F32),
            pltpu.VMEM((2, m, *half), F32),
            pltpu.VMEM((n, width, part), F32),
            pltpu.VMEM((n, width, part), F32),
            pltpu.VMEM((m, width, part), F32),
            pltpu.VMEM((n, width, part), F32),
            pltpu.VMEM((KSTEPS, n, width + 8, part), F32),
            pltpu.VMEM((KSTEPS, n, width + 8, part), F32),
            pltpu.VMEM((KSTEPS, m, width + 8, part), F32),
            pltpu.VMEM((KSTEPS, n, width, part), F32),
            *sems,
        ],
        compiler_params=pltpu.CompilerParams(
            collective_id=0, has_side_effects=True, vmem_limit_bytes=58 * 1024 * 1024
        ),
        name="spectral",
    )(tile_values, tile_rows, tile_columns, tile_count, start_basis, seed_rows[None, :])


def solution(mesh):
    return jax.shard_map(
        local,
        mesh=mesh,
        in_specs=(
            P(("group", "dev"), None, None),
            P(("group", "dev")),
            P(("group", "dev")),
            P(("group", "dev")),
            P(("group", "dev"), None),
            P(),
        ),
        out_specs=(P(("group", "dev"), None), P()),
        check_vma=False,
    )
```

```python
import functools

import jax
import jax.numpy as jnp
from jax import lax
from jax.experimental import pallas as pl
from jax.experimental.pallas import tpu as pltpu
from jax.sharding import PartitionSpec as P

KSTEPS = 2
SHARPNESS = 4.0
MESH = pl.DeviceIdType.MESH
F32 = jnp.float32
HIGHEST = lax.Precision.HIGHEST
NN = (((1,), (0,)), ((), ()))
NT = (((1,), (1,)), ((), ()))


def mm(a, b, dims=NN):
    return lax.dot_general(a, b, dims, precision=HIGHEST, preferred_element_type=F32)


def loop(n, body):
    if n <= 8:
        for i in range(n):
            body(i)
    else:

        def step(i, carry):
            body(i)
            return carry

        lax.fori_loop(0, n, step, 0)


def fold(n, ref):
    if n <= 8:
        total = ref[0]
        for i in range(1, n):
            total = total + ref[i]
        return total
    return lax.fori_loop(1, n, lambda i, total: total + ref[i], ref[0])


class Exchange:
    def __init__(self, axis, n, me, land, sems, source=None):
        self.axis, self.n, self.me = axis, n, me
        self.land, self.source = land, source
        self.send, self.recv = sems

    def copy(self, peer, slot):
        source = self.land(self.me) if self.source is None else self.source(peer)
        return pltpu.make_async_remote_copy(
            src_ref=source,
            dst_ref=self.land(slot),
            send_sem=self.send.at[peer],
            recv_sem=self.recv.at[slot],
            device_id={self.axis: peer},
            device_id_type=MESH,
        )

    def peer(self, i):
        return lax.rem(self.me + 1 + i, self.n)

    def start(self):
        loop(self.n - 1, lambda i: self.copy(self.peer(i), self.me).start())

    def wait_recv(self):
        loop(self.n - 1, lambda i: self.copy(self.peer(i), self.peer(i)).wait_recv())

    def wait_send(self):
        loop(self.n - 1, lambda i: self.copy(self.peer(i), self.me).wait_send())


def factor_inverse(gram):
    k = gram.shape[0]
    rows = lax.broadcasted_iota(jnp.int32, (k, k), 0)
    lanes = lax.broadcasted_iota(jnp.int32, (k, k), 1)
    table = jnp.concatenate([gram, jnp.where(rows == lanes, 1.0, 0.0).astype(F32)], axis=1)
    parts = [table[8 * b : 8 * b + 8] for b in range(k // 8)]
    sub = lax.broadcasted_iota(jnp.int32, (8, 2 * k), 0)
    for i in range(0, k, 2):
        b, r = divmod(i, 8)
        own = parts[b]
        top, low = own[r : r + 1], own[r + 1 : r + 2]
        pivot, cross, corner = (
            jnp.broadcast_to(v, (1, 2 * k))
            for v in (top[:, i : i + 1], top[:, i + 1 : i + 2], low[:, i + 1 : i + 2])
        )
        over = 1.0 / pivot
        ratio = cross * over
        scaled_low = (low - ratio * top) / (corner - ratio * cross)
        scaled_top = (top - cross * scaled_low) * over

        def minus(part):
            return part - part[:, i : i + 1] * scaled_top - part[:, i + 1 : i + 2] * scaled_low

        fixed = jnp.where(sub == r + 1, own - ratio * top, own)
        parts[b] = jnp.where(sub > r + 1, minus(own), fixed) if r < 6 else fixed
        for c in range(b + 1, k // 8):
            parts[c] = minus(parts[c])
    table = jnp.concatenate(parts, axis=0)
    diag = jnp.sum(jnp.where(rows == lanes, table[:, :k], 0.0), axis=1, keepdims=True)
    return table[:, k:] / jnp.sqrt(diag)


def pack(gram):
    half = gram.shape[0] // 2
    return jnp.concatenate([gram[:half], gram[half:]], axis=1)


def unpack(packed):
    k = packed.shape[1] // 2
    return jnp.concatenate([packed[:, :k], packed[:, k:]], axis=0)


def kernel(
    n, m, total_rows,
    tiles, rows_ref, columns_ref, count_ref, start, seeds,
    unit_out, centres_out,
    matrix, basis0, basis1, images, gram_dev, gram_group,
    seed_out, seed_dev, seed_group, seed_all,
    *rest,
):
    me, g = lax.axis_index("dev"), lax.axis_index("group")
    k_out, k_dev, k_group, k_all = (rest[2 * i : 2 * i + 2] for i in range(4))
    sems = rest[8:]
    pairs = [(sems[2 * i], sems[2 * i + 1]) for i in range(len(sems) // 2)]
    slots, block = tiles.shape[0], tiles.shape[1]
    width, local_rows = start.shape
    row_blocks = local_rows // block
    clusters = seeds.shape[1]
    part = clusters // n

    barrier = pltpu.get_barrier_semaphore()
    for axis, size, index in (("dev", n, me), ("group", m, g)):
        loop(
            size - 1,
            lambda i: pl.semaphore_signal(
                barrier, inc=1, device_id={axis: lax.rem(index + 1 + i, size)}, device_id_type=MESH
            ),
        )
    for r in range(row_blocks):
        basis0[me * row_blocks + r] = start[:, r * block : (r + 1) * block]
    pl.semaphore_wait(barrier, n - 1 + m - 1)

    used = iter(pairs)
    pending = []

    def exchange(axis, land, source=None):
        size, index = (n, me) if axis == "dev" else (m, g)
        made = Exchange(axis, size, index, land, next(used), source)
        made.start()
        pending.append(made)
        return made

    own_blocks = lambda d: basis0.at[pl.ds(d * row_blocks, row_blocks)]
    gather = exchange("dev", own_blocks)
    count = count_ref[0]
    for s in range(slots):
        for r in range(row_blocks):
            keep = jnp.logical_and(rows_ref[s] == r, s < count)
            matrix[r * block : (r + 1) * block, s * block : (s + 1) * block] = tiles[s] * jnp.where(
                keep, 1.0, 0.0
            ).astype(jnp.bfloat16)

    def apply(basis):
        picked = jnp.concatenate([basis[columns_ref[s]] for s in range(slots)], axis=1)
        return lax.dot_general(picked, matrix[...], NT, preferred_element_type=F32)

    def start_gram(image, turn):
        gram_dev[turn, me] = pack(mm(image, image, NT))
        return exchange("dev", lambda d: gram_dev.at[turn, d])

    def end_gram(first, turn):
        first.wait_recv()
        gram_group[turn, g] = fold(n, gram_dev.at[turn])
        return exchange("group", lambda d: gram_group.at[turn, d])

    gather.wait_recv()
    image = apply(basis0)
    first = start_gram(image, 0)
    images[me] = image
    gather = exchange("dev", lambda d: images.at[d])
    second = end_gram(first, 0)
    second.wait_recv()
    inverse = factor_inverse(unpack(fold(m, gram_group.at[0])))
    gather.wait_recv()

    def solve(d):
        solved = mm(inverse, images[d])
        for r in range(row_blocks):
            basis1[d * row_blocks + r] = solved[:, r * block : (r + 1) * block].astype(jnp.bfloat16)

    loop(n, solve)
    image = apply(basis1)
    first = start_gram(image, 1)

    half = width // 2

    def split(values, out, extra=None):
        for h in range(2):
            for c in range(n):
                lanes = slice(c * part, (c + 1) * part)
                out[h][c, :half] = values[h * half : (h + 1) * half, lanes]
                if h == 0 and extra is not None:
                    out[h][c, half:] = jnp.broadcast_to(extra[:, lanes], (8, part))

    def join(refs):
        return jnp.concatenate(
            [jnp.concatenate([ref[c] for c in range(n)], axis=1) for ref in refs], axis=0
        )

    def start_dev(out, dev):
        made = []
        for h in range(2):
            dev[h][me] = out[h][me]
            made.append(
                exchange("dev", lambda d, h=h: dev[h].at[d], lambda p, h=h: out[h].at[p])
            )
        return made

    def start_group(made, dev, group):
        after = []
        for h in range(2):
            made[h].wait_recv()
            group[h][g] = fold(n, dev[h])
            after.append(exchange("group", lambda d, h=h: group[h].at[d]))
        return after

    def start_all(made, group, every, finish):
        after = []
        for h in range(2):
            made[h].wait_recv()
            every[h][me] = finish(h, fold(m, group[h]))
            after.append(exchange("dev", lambda d, h=h: every[h].at[d]))
        return after

    first_row = (g * n + me) * local_rows
    chooser = jnp.where(
        lax.broadcasted_iota(jnp.int32, (local_rows, clusters), 0) == seeds[...] - first_row, 1.0, 0.0
    ).astype(F32)
    seed_out, seed_dev, seed_group, seed_all = (
        [ref.at[h] for h in range(2)] for ref in (seed_out, seed_dev, seed_group, seed_all)
    )
    split(mm(image, chooser), seed_out)
    made = start_dev(seed_out, seed_dev)
    second = end_gram(first, 1)
    made = start_group(made, seed_dev, seed_group)
    second.wait_recv()
    inverse = factor_inverse(unpack(fold(m, gram_group.at[1])))
    made = start_all(made, seed_group, seed_all, lambda h, total: total)

    def normalise(image_t):
        embedding = mm(inverse, image_t) * jnp.sqrt(F32(total_rows))
        return embedding / jnp.sqrt(jnp.sum(embedding * embedding, axis=0, keepdims=True) + 1e-06)

    unit_t = normalise(image)
    unit = unit_t.T
    unit_out[...] = unit_t
    unit_square = jnp.sum(unit * unit, axis=1, keepdims=True)
    for gather in made:
        gather.wait_recv()
    centres = normalise(join(seed_all))
    for turn in range(KSTEPS):
        dist = unit_square - 2.0 * mm(unit, centres) + jnp.sum(centres * centres, axis=0, keepdims=True)
        weights = jnp.exp(-SHARPNESS * dist)
        member = weights / jnp.sum(weights, axis=1, keepdims=True)
        out, dev, group, every = (
            [ref.at[turn] for ref in refs] for refs in (k_out, k_dev, k_group, k_all)
        )
        split(mm(unit_t, member), out, jnp.sum(member, axis=0, keepdims=True))
        made = start_group(start_dev(out, dev), dev, group)
        mass = []

        def finish(h, total):
            if h == 0:
                mass.append(total[half : half + 1])
            return total[:half] / mass[0]

        for gather in start_all(made, group, every, finish):
            gather.wait_recv()
        centres = join(every)
    centres_out[...] = centres
    for made in pending:
        made.wait_send()


def local(tile_values, tile_rows, tile_columns, tile_count, start_basis, seed_rows):
    n, m = lax.axis_size("dev"), lax.axis_size("group")
    slots, block = tile_values.shape[0], tile_values.shape[1]
    local_rows, width = start_basis.shape
    row_blocks = local_rows // block
    clusters = seed_rows.shape[0]
    part = clusters // n
    vmem = pl.BlockSpec(memory_space=pltpu.VMEM)
    smem = pl.BlockSpec(memory_space=pltpu.SMEM)
    half = (width // 2, 2 * width)
    axes = ["dev", "dev", "dev", "group", "dev", "dev", "dev", "group", "group", "group", "dev", "dev"]
    axes += ["dev", "dev", "group", "group", "dev", "dev"] * KSTEPS
    sems = []
    for axis in axes:
        sems += [pltpu.SemaphoreType.DMA((n if axis == "dev" else m,))] * 2
    unit, centres = pl.pallas_call(
        functools.partial(kernel, n, m, local_rows * n * m),
        out_shape=(
            jax.ShapeDtypeStruct((width, local_rows), F32),
            jax.ShapeDtypeStruct((width, clusters), F32),
        ),
        in_specs=[vmem, smem, smem, smem, vmem, vmem],
        out_specs=(vmem, vmem),
        scratch_shapes=[
            pltpu.VMEM((local_rows, slots * block), jnp.bfloat16),
            pltpu.VMEM((n * row_blocks, width, block), jnp.bfloat16),
            pltpu.VMEM((n * row_blocks, width, block), jnp.bfloat16),
            pltpu.VMEM((n, width, local_rows), F32),
            pltpu.VMEM((2, n, *half), F32),
            pltpu.VMEM((2, m, *half), F32),
            *[pltpu.VMEM((2, size, width // 2, part), F32) for size in (n, n, m, n)],
            *[
                pltpu.VMEM((KSTEPS, size, width // 2 + more, part), F32)
                for size, extra in ((n, 8), (n, 8), (m, 8), (n, 0))
                for more in (extra, 0)
            ],
            *sems,
        ],
        compiler_params=pltpu.CompilerParams(
            collective_id=0, has_side_effects=True, vmem_limit_bytes=58 * 1024 * 1024
        ),
        name="spectral",
    )(tile_values, tile_rows, tile_columns, tile_count, start_basis.T, seed_rows[None, :])
    return unit.T, centres.T


def solution(mesh):
    return jax.shard_map(
        local,
        mesh=mesh,
        in_specs=(
            P(("group", "dev"), None, None),
            P(("group", "dev")),
            P(("group", "dev")),
            P(("group", "dev")),
            P(("group", "dev"), None),
            P(),
        ),
        out_specs=(P(("group", "dev"), None), P()),
        check_vma=False,
    )
```

```python
import functools

import jax
import jax.numpy as jnp
from jax import lax
from jax.experimental import pallas as pl
from jax.experimental.pallas import tpu as pltpu
from jax.sharding import PartitionSpec as P

KSTEPS = 2
SHARPNESS = 4.0
MASS_ROWS = 16
MESH = pl.DeviceIdType.MESH
F32 = jnp.float32
HIGHEST = lax.Precision.HIGHEST
NN = (((1,), (0,)), ((), ()))
NT = (((1,), (1,)), ((), ()))


def mm(a, b, dims=NN):
    return lax.dot_general(a, b, dims, precision=HIGHEST, preferred_element_type=F32)


def high_low(x):
    high = x.astype(jnp.bfloat16)
    return high, (x - high.astype(F32)).astype(jnp.bfloat16)


def dot16(a, b):
    return lax.dot_general(a, b, NN, preferred_element_type=F32)


def loop(n, body):
    if n <= 8:
        for i in range(n):
            body(i)
    else:

        def step(i, carry):
            body(i)
            return carry

        lax.fori_loop(0, n, step, 0)


def fold(n, ref):
    total = ref[0].astype(F32)
    if n <= 8:
        for i in range(1, n):
            total = total + ref[i].astype(F32)
        return total
    return lax.fori_loop(1, n, lambda i, total: total + ref[i].astype(F32), total)


class Exchange:
    def __init__(self, axis, n, me, land, sems, source=None):
        self.axis, self.n, self.me = axis, n, me
        self.land, self.source = land, source
        self.send, self.recv = sems

    def copy(self, peer, slot):
        source = self.land(self.me) if self.source is None else self.source(peer)
        return pltpu.make_async_remote_copy(
            src_ref=source,
            dst_ref=self.land(slot),
            send_sem=self.send.at[peer],
            recv_sem=self.recv.at[slot],
            device_id={self.axis: peer},
            device_id_type=MESH,
        )

    def peer(self, i):
        return lax.rem(self.me + 1 + i, self.n)

    def start(self):
        loop(self.n - 1, lambda i: self.copy(self.peer(i), self.me).start())

    def wait_recv(self):
        loop(self.n - 1, lambda i: self.copy(self.peer(i), self.peer(i)).wait_recv())

    def wait_send(self):
        loop(self.n - 1, lambda i: self.copy(self.peer(i), self.me).wait_send())


def factor_inverse(gram):
    k = gram.shape[0]
    rows = lax.broadcasted_iota(jnp.int32, (k, k), 0)
    lanes = lax.broadcasted_iota(jnp.int32, (k, k), 1)
    table = jnp.concatenate([gram, jnp.where(rows == lanes, 1.0, 0.0).astype(F32)], axis=1)
    parts = [table[8 * b : 8 * b + 8] for b in range(k // 8)]
    sub = lax.broadcasted_iota(jnp.int32, (8, 2 * k), 0)
    for i in range(0, k, 2):
        b, r = divmod(i, 8)
        own = parts[b]
        top, low = own[r : r + 1], own[r + 1 : r + 2]
        pivot, cross, corner = (
            jnp.broadcast_to(v, (1, 2 * k))
            for v in (top[:, i : i + 1], top[:, i + 1 : i + 2], low[:, i + 1 : i + 2])
        )
        over = 1.0 / pivot
        ratio = cross * over
        scaled_low = (low - ratio * top) / (corner - ratio * cross)
        scaled_top = (top - cross * scaled_low) * over

        def minus(part):
            return part - part[:, i : i + 1] * scaled_top - part[:, i + 1 : i + 2] * scaled_low

        fixed = jnp.where(sub == r + 1, own - ratio * top, own)
        parts[b] = jnp.where(sub > r + 1, minus(own), fixed) if r < 6 else fixed
        for c in range(b + 1, k // 8):
            parts[c] = minus(parts[c])
    table = jnp.concatenate(parts, axis=0)
    diag = jnp.sum(jnp.where(rows == lanes, table[:, :k], 0.0), axis=1, keepdims=True)
    return table[:, k:] / jnp.sqrt(diag)


def pack(gram):
    half = gram.shape[0] // 2
    return jnp.concatenate([gram[:half], gram[half:]], axis=1)


def unpack(packed):
    k = packed.shape[1] // 2
    return jnp.concatenate([packed[:, :k], packed[:, k:]], axis=0)


def kernel(
    n, m, total_rows,
    tiles, rows_ref, columns_ref, count_ref, start, seeds,
    unit_out, centres_out,
    matrix, basis0, basis1, images, gram_dev, gram_group,
    seed_out, seed_dev, seed_group, seed_all,
    *rest,
):
    me, g = lax.axis_index("dev"), lax.axis_index("group")
    k_out, k_dev, k_group, k_all = (rest[2 * i : 2 * i + 2] for i in range(4))
    sems = rest[8:]
    pairs = [(sems[2 * i], sems[2 * i + 1]) for i in range(len(sems) // 2)]
    slots, block = tiles.shape[0], tiles.shape[1]
    width, local_rows = start.shape
    row_blocks = local_rows // block
    clusters = seeds.shape[1]
    part = clusters // n

    barrier = pltpu.get_barrier_semaphore()
    for axis, size, index in (("dev", n, me), ("group", m, g)):
        loop(
            size - 1,
            lambda i: pl.semaphore_signal(
                barrier, inc=1, device_id={axis: lax.rem(index + 1 + i, size)}, device_id_type=MESH
            ),
        )
    for r in range(row_blocks):
        basis0[me * row_blocks + r] = start[:, r * block : (r + 1) * block]
    pl.semaphore_wait(barrier, n - 1 + m - 1)

    used = iter(pairs)
    pending = []

    def exchange(axis, land, source=None):
        size, index = (n, me) if axis == "dev" else (m, g)
        made = Exchange(axis, size, index, land, next(used), source)
        made.start()
        pending.append(made)
        return made

    own_blocks = lambda d: basis0.at[pl.ds(d * row_blocks, row_blocks)]
    gather = exchange("dev", own_blocks)
    count = count_ref[0]
    for s in range(slots):
        for r in range(row_blocks):
            keep = jnp.logical_and(rows_ref[s] == r, s < count)
            matrix[r * block : (r + 1) * block, s * block : (s + 1) * block] = tiles[s] * jnp.where(
                keep, 1.0, 0.0
            ).astype(jnp.bfloat16)

    def apply(basis):
        picked = jnp.concatenate([basis[columns_ref[s]] for s in range(slots)], axis=1)
        return lax.dot_general(picked, matrix[...], NT, preferred_element_type=F32)

    def start_gram(image, turn):
        gram_dev[turn, me] = pack(mm(image, image, NT))
        return exchange("dev", lambda d: gram_dev.at[turn, d])

    def end_gram(first, turn):
        first.wait_recv()
        gram_group[turn, g] = fold(n, gram_dev.at[turn])
        return exchange("group", lambda d: gram_group.at[turn, d])

    gather.wait_recv()
    image = apply(basis0)
    first = start_gram(image, 0)
    images[me] = image
    gather = exchange("dev", lambda d: images.at[d])
    second = end_gram(first, 0)
    second.wait_recv()
    inverse = factor_inverse(unpack(fold(m, gram_group.at[0])))
    gather.wait_recv()

    def solve(d):
        solved = mm(inverse, images[d])
        for r in range(row_blocks):
            basis1[d * row_blocks + r] = solved[:, r * block : (r + 1) * block].astype(jnp.bfloat16)

    loop(n, solve)
    image = apply(basis1)
    first = start_gram(image, 1)

    half = width // 2

    def split(values, out, extra=None):
        for h in range(2):
            for c in range(n):
                lanes = slice(c * part, (c + 1) * part)
                out[h][c, :half] = values[h * half : (h + 1) * half, lanes].astype(out[h].dtype)
                if h == 0 and extra is not None:
                    out[h][c, half:] = jnp.broadcast_to(
                        extra[:, lanes], (MASS_ROWS, part)
                    ).astype(out[h].dtype)

    def join(refs):
        return jnp.concatenate(
            [jnp.concatenate([ref[c] for c in range(n)], axis=1) for ref in refs], axis=0
        )

    def start_dev(out, dev):
        made = []
        for h in range(2):
            dev[h][me] = out[h][me]
            made.append(
                exchange("dev", lambda d, h=h: dev[h].at[d], lambda p, h=h: out[h].at[p])
            )
        return made

    def start_group(made, dev, group):
        after = []
        for h in range(2):
            made[h].wait_recv()
            total = fold(n, dev[h])
            group[h][g] = total[: group[h].shape[1]]
            after.append(exchange("group", lambda d, h=h: group[h].at[d]))
        return after

    def start_all(made, group, every, finish):
        after = []
        for h in range(2):
            made[h].wait_recv()
            every[h][me] = finish(h, fold(m, group[h]))
            after.append(exchange("dev", lambda d, h=h: every[h].at[d]))
        return after

    first_row = (g * n + me) * local_rows
    chooser = jnp.where(
        lax.broadcasted_iota(jnp.int32, (local_rows, clusters), 0) == seeds[...] - first_row, 1.0, 0.0
    ).astype(jnp.bfloat16)
    high = image.astype(jnp.bfloat16)
    rest_of = image - high.astype(F32)
    pieces = dot16(jnp.concatenate([high, *high_low(rest_of)], axis=0), chooser)
    seed_out, seed_dev, seed_group, seed_all = (
        [ref.at[h] for h in range(2)] for ref in (seed_out, seed_dev, seed_group, seed_all)
    )
    split(pieces[:width] + pieces[width : 2 * width] + pieces[2 * width :], seed_out)
    made = start_dev(seed_out, seed_dev)
    second = end_gram(first, 1)
    made = start_group(made, seed_dev, seed_group)
    second.wait_recv()
    inverse = factor_inverse(unpack(fold(m, gram_group.at[1])))
    made = start_all(made, seed_group, seed_all, lambda h, total: total)

    def normalise(image_t):
        embedding = mm(inverse, image_t) * jnp.sqrt(F32(total_rows))
        return embedding / jnp.sqrt(jnp.sum(embedding * embedding, axis=0, keepdims=True) + 1e-06)

    unit_t = normalise(image)
    unit_out[...] = unit_t
    unit = unit_t.T
    unit_square = jnp.sum(unit * unit, axis=1, keepdims=True)
    unit_high, unit_low = high_low(unit_t)
    left = jnp.concatenate([unit_high, unit_low, unit_high], axis=0).astype(F32).T.astype(jnp.bfloat16)
    unit_pair = jnp.concatenate([unit_high, unit_low], axis=0)
    for gather in made:
        gather.wait_recv()
    centres = normalise(join(seed_all))
    for turn in range(KSTEPS):
        high, low = high_low(centres)
        inner = dot16(left, jnp.concatenate([high, high, low], axis=0))
        dist = unit_square - 2.0 * inner + jnp.sum(centres * centres, axis=0, keepdims=True)
        weights = jnp.exp(-SHARPNESS * dist)
        member = weights / jnp.sum(weights, axis=1, keepdims=True)
        out, dev, group, every = (
            [ref.at[turn] for ref in refs] for refs in (k_out, k_dev, k_group, k_all)
        )
        high, low = high_low(member)
        pair = dot16(unit_pair, high)
        split(pair[:width] + pair[width:] + dot16(unit_high, low), out, jnp.sum(member, axis=0, keepdims=True))
        made = start_group(start_dev(out, dev), dev, group)
        mass = []

        def finish(h, total):
            if h == 0:
                mass.append(total[half : half + 1])
            return total[:half] / mass[0]

        for gather in start_all(made, group, every, finish):
            gather.wait_recv()
        centres = join(every)
    centres_out[...] = centres
    for made in pending:
        made.wait_send()


def local(tile_values, tile_rows, tile_columns, tile_count, start_basis, seed_rows):
    n, m = lax.axis_size("dev"), lax.axis_size("group")
    slots, block = tile_values.shape[0], tile_values.shape[1]
    local_rows, width = start_basis.shape
    row_blocks = local_rows // block
    clusters = seed_rows.shape[0]
    part = clusters // n
    vmem = pl.BlockSpec(memory_space=pltpu.VMEM)
    smem = pl.BlockSpec(memory_space=pltpu.SMEM)
    half = (width // 2, 2 * width)
    axes = ["dev", "dev", "dev", "group", "dev", "dev", "dev", "group", "group", "group", "dev", "dev"]
    axes += ["dev", "dev", "group", "group", "dev", "dev"] * KSTEPS
    sems = []
    for axis in axes:
        sems += [pltpu.SemaphoreType.DMA((n if axis == "dev" else m,))] * 2
    unit, centres = pl.pallas_call(
        functools.partial(kernel, n, m, local_rows * n * m),
        out_shape=(
            jax.ShapeDtypeStruct((width, local_rows), F32),
            jax.ShapeDtypeStruct((width, clusters), F32),
        ),
        in_specs=[vmem, smem, smem, smem, vmem, vmem],
        out_specs=(vmem, vmem),
        scratch_shapes=[
            pltpu.VMEM((local_rows, slots * block), jnp.bfloat16),
            pltpu.VMEM((n * row_blocks, width, block), jnp.bfloat16),
            pltpu.VMEM((n * row_blocks, width, block), jnp.bfloat16),
            pltpu.VMEM((n, width, local_rows), F32),
            pltpu.VMEM((2, n, *half), F32),
            pltpu.VMEM((2, m, *half), F32),
            *[pltpu.VMEM((2, size, width // 2, part), F32) for size in (n, n, m, n)],
            *[
                pltpu.VMEM((KSTEPS, size, width // 2 + more, part), kind)
                for size, extra, kind in (
                    (n, MASS_ROWS, jnp.bfloat16),
                    (n, MASS_ROWS, jnp.bfloat16),
                    (m, 8, F32),
                    (n, 0, F32),
                )
                for more in (extra, 0)
            ],
            *sems,
        ],
        compiler_params=pltpu.CompilerParams(
            collective_id=0, has_side_effects=True, vmem_limit_bytes=58 * 1024 * 1024
        ),
        name="spectral",
    )(tile_values, tile_rows, tile_columns, tile_count, start_basis.T, seed_rows[None, :])
    return unit.T, centres.T


def solution(mesh):
    return jax.shard_map(
        local,
        mesh=mesh,
        in_specs=(
            P(("group", "dev"), None, None),
            P(("group", "dev")),
            P(("group", "dev")),
            P(("group", "dev")),
            P(("group", "dev"), None),
            P(),
        ),
        out_specs=(P(("group", "dev"), None), P()),
        check_vma=False,
    )
```

```python
import functools

import jax
import jax.numpy as jnp
from jax import lax
from jax.experimental import pallas as pl
from jax.experimental.pallas import tpu as pltpu
from jax.sharding import PartitionSpec as P

KSTEPS = 2
SHARPNESS = 4.0
MASS_ROWS = 16
MESH = pl.DeviceIdType.MESH
F32 = jnp.float32
HIGHEST = lax.Precision.HIGHEST
NN = (((1,), (0,)), ((), ()))
NT = (((1,), (1,)), ((), ()))


def mm(a, b, dims=NN):
    return lax.dot_general(a, b, dims, precision=HIGHEST, preferred_element_type=F32)


def high_low(x):
    high = x.astype(jnp.bfloat16)
    return high, (x - high.astype(F32)).astype(jnp.bfloat16)


def dot16(a, b):
    return lax.dot_general(a, b, NN, preferred_element_type=F32)


def loop(n, body):
    if n <= 8:
        for i in range(n):
            body(i)
    else:

        def step(i, carry):
            body(i)
            return carry

        lax.fori_loop(0, n, step, 0)


def fold(n, ref):
    total = ref[0].astype(F32)
    if n <= 8:
        for i in range(1, n):
            total = total + ref[i].astype(F32)
        return total
    return lax.fori_loop(1, n, lambda i, total: total + ref[i].astype(F32), total)


class Exchange:
    def __init__(self, axis, n, me, land, sems, source=None):
        self.axis, self.n, self.me = axis, n, me
        self.land, self.source = land, source
        self.send, self.recv = sems

    def copy(self, peer, slot):
        source = self.land(self.me) if self.source is None else self.source(peer)
        return pltpu.make_async_remote_copy(
            src_ref=source,
            dst_ref=self.land(slot),
            send_sem=self.send.at[peer],
            recv_sem=self.recv.at[slot],
            device_id={self.axis: peer},
            device_id_type=MESH,
        )

    def peer(self, i):
        return lax.rem(self.me + 1 + i, self.n)

    def start(self):
        loop(self.n - 1, lambda i: self.copy(self.peer(i), self.me).start())

    def wait_recv(self):
        loop(self.n - 1, lambda i: self.copy(self.peer(i), self.peer(i)).wait_recv())

    def wait_send(self):
        loop(self.n - 1, lambda i: self.copy(self.peer(i), self.me).wait_send())


def factor_inverse(gram):
    k = gram.shape[0]
    rows = lax.broadcasted_iota(jnp.int32, (k, k), 0)
    lanes = lax.broadcasted_iota(jnp.int32, (k, k), 1)
    table = jnp.concatenate([gram, jnp.where(rows == lanes, 1.0, 0.0).astype(F32)], axis=1)
    parts = [table[8 * b : 8 * b + 8] for b in range(k // 8)]
    sub = lax.broadcasted_iota(jnp.int32, (8, 2 * k), 0)
    for i in range(0, k, 2):
        b, r = divmod(i, 8)
        own = parts[b]
        top, low = own[r : r + 1], own[r + 1 : r + 2]
        pivot, cross, corner = (
            jnp.broadcast_to(v, (1, 2 * k))
            for v in (top[:, i : i + 1], top[:, i + 1 : i + 2], low[:, i + 1 : i + 2])
        )
        over = 1.0 / pivot
        ratio = cross * over
        scaled_low = (low - ratio * top) / (corner - ratio * cross)
        scaled_top = (top - cross * scaled_low) * over

        def minus(part):
            return part - part[:, i : i + 1] * scaled_top - part[:, i + 1 : i + 2] * scaled_low

        fixed = jnp.where(sub == r + 1, own - ratio * top, own)
        parts[b] = jnp.where(sub > r + 1, minus(own), fixed) if r < 6 else fixed
        for c in range(b + 1, k // 8):
            parts[c] = minus(parts[c])
    table = jnp.concatenate(parts, axis=0)
    diag = jnp.sum(jnp.where(rows == lanes, table[:, :k], 0.0), axis=1, keepdims=True)
    return table[:, k:] / jnp.sqrt(diag)


def pack(gram):
    half = gram.shape[0] // 2
    return jnp.concatenate([gram[:half], gram[half:]], axis=1)


def unpack(packed):
    k = packed.shape[1] // 2
    return jnp.concatenate([packed[:, :k], packed[:, k:]], axis=0)


def kernel(
    n, m, total_rows,
    tiles, rows_ref, columns_ref, count_ref, start, seeds,
    unit_out, centres_out,
    matrix, basis0, basis1, images, gram_dev, gram_group,
    seed_out, seed_dev, seed_group, seed_all,
    *rest,
):
    me, g = lax.axis_index("dev"), lax.axis_index("group")
    k_out, k_dev, k_group, k_all, k_early = (rest[2 * i : 2 * i + 2] for i in range(5))
    sems = rest[10:]
    pairs = [(sems[2 * i], sems[2 * i + 1]) for i in range(len(sems) // 2)]
    slots, block = tiles.shape[0], tiles.shape[1]
    width, local_rows = start.shape
    row_blocks = local_rows // block
    clusters = seeds.shape[1]
    part = clusters // n

    barrier = pltpu.get_barrier_semaphore()
    for axis, size, index in (("dev", n, me), ("group", m, g)):
        loop(
            size - 1,
            lambda i: pl.semaphore_signal(
                barrier, inc=1, device_id={axis: lax.rem(index + 1 + i, size)}, device_id_type=MESH
            ),
        )
    for r in range(row_blocks):
        basis0[me * row_blocks + r] = start[:, r * block : (r + 1) * block]
    pl.semaphore_wait(barrier, n - 1 + m - 1)

    used = iter(pairs)
    pending = []

    def exchange(axis, land, source=None):
        size, index = (n, me) if axis == "dev" else (m, g)
        made = Exchange(axis, size, index, land, next(used), source)
        made.start()
        pending.append(made)
        return made

    own_blocks = lambda d: basis0.at[pl.ds(d * row_blocks, row_blocks)]
    gather = exchange("dev", own_blocks)
    count = count_ref[0]
    for s in range(slots):
        for r in range(row_blocks):
            keep = jnp.logical_and(rows_ref[s] == r, s < count)
            matrix[r * block : (r + 1) * block, s * block : (s + 1) * block] = tiles[s] * jnp.where(
                keep, 1.0, 0.0
            ).astype(jnp.bfloat16)

    def apply(basis):
        picked = jnp.concatenate([basis[columns_ref[s]] for s in range(slots)], axis=1)
        return lax.dot_general(picked, matrix[...], NT, preferred_element_type=F32)

    def start_gram(image, turn):
        gram_dev[turn, me] = pack(mm(image, image, NT))
        return exchange("dev", lambda d: gram_dev.at[turn, d])

    def end_gram(first, turn):
        first.wait_recv()
        gram_group[turn, g] = fold(n, gram_dev.at[turn])
        return exchange("group", lambda d: gram_group.at[turn, d])

    gather.wait_recv()
    image = apply(basis0)
    first = start_gram(image, 0)
    images[me] = image
    gather = exchange("dev", lambda d: images.at[d])
    second = end_gram(first, 0)
    second.wait_recv()
    inverse = factor_inverse(unpack(fold(m, gram_group.at[0])))
    gather.wait_recv()

    def solve(d):
        solved = mm(inverse, images[d])
        for r in range(row_blocks):
            basis1[d * row_blocks + r] = solved[:, r * block : (r + 1) * block].astype(jnp.bfloat16)

    loop(n, solve)
    image = apply(basis1)
    first = start_gram(image, 1)

    half = width // 2

    def split(values, out, extra=None):
        for h in range(2):
            for c in range(n):
                lanes = slice(c * part, (c + 1) * part)
                out[h][c, :half] = values[h * half : (h + 1) * half, lanes].astype(out[h].dtype)
                if h == 0 and extra is not None:
                    out[h][c, half:] = jnp.broadcast_to(
                        extra[:, lanes], (MASS_ROWS, part)
                    ).astype(out[h].dtype)

    def join(refs):
        return jnp.concatenate(
            [jnp.concatenate([ref[c] for c in range(n)], axis=1) for ref in refs], axis=0
        )

    def start_dev(out, dev):
        made = []
        for h in range(2):
            dev[h][me] = out[h][me]
            made.append(
                exchange("dev", lambda d, h=h: dev[h].at[d], lambda p, h=h: out[h].at[p])
            )
        return made

    def start_group(made, dev, group):
        after = []
        for h in range(2):
            made[h].wait_recv()
            total = fold(n, dev[h])
            group[h][g] = total[: group[h].shape[1]].astype(group[h].dtype)
            after.append(exchange("group", lambda d, h=h: group[h].at[d]))
        return after

    def start_all(made, group, every, finish):
        after = []
        for h in range(2):
            made[h].wait_recv()
            every[h][me] = finish(h, fold(m, group[h]))
            after.append(exchange("dev", lambda d, h=h: every[h].at[d]))
        return after

    first_row = (g * n + me) * local_rows
    chooser = jnp.where(
        lax.broadcasted_iota(jnp.int32, (local_rows, clusters), 0) == seeds[...] - first_row, 1.0, 0.0
    ).astype(jnp.bfloat16)
    high = image.astype(jnp.bfloat16)
    rest_of = image - high.astype(F32)
    pieces = dot16(jnp.concatenate([high, *high_low(rest_of)], axis=0), chooser)
    seed_out, seed_dev, seed_group, seed_all = (
        [ref.at[h] for h in range(2)] for ref in (seed_out, seed_dev, seed_group, seed_all)
    )
    split(pieces[:width] + pieces[width : 2 * width] + pieces[2 * width :], seed_out)
    made = start_dev(seed_out, seed_dev)
    second = end_gram(first, 1)
    made = start_group(made, seed_dev, seed_group)
    second.wait_recv()
    inverse = factor_inverse(unpack(fold(m, gram_group.at[1])))
    made = start_all(made, seed_group, seed_all, lambda h, total: total)

    def normalise(image_t):
        embedding = mm(inverse, image_t) * jnp.sqrt(F32(total_rows))
        return embedding / jnp.sqrt(jnp.sum(embedding * embedding, axis=0, keepdims=True) + 1e-06)

    unit_t = normalise(image)
    unit_out[...] = unit_t
    unit = unit_t.T
    unit_square = jnp.sum(unit * unit, axis=1, keepdims=True)
    unit_high, unit_low = high_low(unit_t)
    left = jnp.concatenate([unit_high, unit_low, unit_high], axis=0).astype(F32).T.astype(jnp.bfloat16)
    unit_pair = jnp.concatenate([unit_high, unit_low], axis=0)
    for gather in made:
        gather.wait_recv()
    centres = normalise(join(seed_all))
    for turn in range(KSTEPS):
        high, low = high_low(centres)
        inner = dot16(left, jnp.concatenate([high, high, low], axis=0))
        dist = unit_square - 2.0 * inner + jnp.sum(centres * centres, axis=0, keepdims=True)
        weights = jnp.exp(-SHARPNESS * dist)
        member = weights / jnp.sum(weights, axis=1, keepdims=True)
        out, dev, group, every = (
            [ref.at[turn] for ref in refs]
            for refs in (k_out, k_dev, k_group if turn + 1 == KSTEPS else k_early, k_all)
        )
        high, low = high_low(member)
        pair = dot16(unit_pair, high)
        split(pair[:width] + pair[width:] + dot16(unit_high, low), out, jnp.sum(member, axis=0, keepdims=True))
        made = start_group(start_dev(out, dev), dev, group)
        mass = []

        def finish(h, total):
            if h == 0:
                mass.append(total[half : half + 1])
            return total[:half] / mass[0]

        for gather in start_all(made, group, every, finish):
            gather.wait_recv()
        centres = join(every)
    centres_out[...] = centres
    for made in pending:
        made.wait_send()


def local(tile_values, tile_rows, tile_columns, tile_count, start_basis, seed_rows):
    n, m = lax.axis_size("dev"), lax.axis_size("group")
    slots, block = tile_values.shape[0], tile_values.shape[1]
    local_rows, width = start_basis.shape
    row_blocks = local_rows // block
    clusters = seed_rows.shape[0]
    part = clusters // n
    vmem = pl.BlockSpec(memory_space=pltpu.VMEM)
    smem = pl.BlockSpec(memory_space=pltpu.SMEM)
    half = (width // 2, 2 * width)
    axes = ["dev", "dev", "dev", "group", "dev", "dev", "dev", "group", "group", "group", "dev", "dev"]
    axes += ["dev", "dev", "group", "group", "dev", "dev"] * KSTEPS
    sems = []
    for axis in axes:
        sems += [pltpu.SemaphoreType.DMA((n if axis == "dev" else m,))] * 2
    unit, centres = pl.pallas_call(
        functools.partial(kernel, n, m, local_rows * n * m),
        out_shape=(
            jax.ShapeDtypeStruct((width, local_rows), F32),
            jax.ShapeDtypeStruct((width, clusters), F32),
        ),
        in_specs=[vmem, smem, smem, smem, vmem, vmem],
        out_specs=(vmem, vmem),
        scratch_shapes=[
            pltpu.VMEM((local_rows, slots * block), jnp.bfloat16),
            pltpu.VMEM((n * row_blocks, width, block), jnp.bfloat16),
            pltpu.VMEM((n * row_blocks, width, block), jnp.bfloat16),
            pltpu.VMEM((n, width, local_rows), F32),
            pltpu.VMEM((2, n, *half), F32),
            pltpu.VMEM((2, m, *half), F32),
            *[pltpu.VMEM((2, size, width // 2, part), F32) for size in (n, n, m, n)],
            *[
                pltpu.VMEM((KSTEPS, size, width // 2 + more, part), kind)
                for size, extra, kind in (
                    (n, MASS_ROWS, jnp.bfloat16),
                    (n, MASS_ROWS, jnp.bfloat16),
                    (m, 8, F32),
                    (n, 0, F32),
                    (m, MASS_ROWS, jnp.bfloat16),
                )
                for more in (extra, 0)
            ],
            *sems,
        ],
        compiler_params=pltpu.CompilerParams(
            collective_id=0, has_side_effects=True, vmem_limit_bytes=58 * 1024 * 1024
        ),
        name="spectral",
    )(tile_values, tile_rows, tile_columns, tile_count, start_basis.T, seed_rows[None, :])
    return unit.T, centres.T


def solution(mesh):
    return jax.shard_map(
        local,
        mesh=mesh,
        in_specs=(
            P(("group", "dev"), None, None),
            P(("group", "dev")),
            P(("group", "dev")),
            P(("group", "dev")),
            P(("group", "dev"), None),
            P(),
        ),
        out_specs=(P(("group", "dev"), None), P()),
        check_vma=False,
    )
```
